32 devices in a mesh: sx: 16 (over z, y, x), sy: 2 (over core).
Axes of the slice: x: 2, y: 2, z: 4, core: 2. Of those that a mesh axis runs over, the one named last changes fastest.
Arguments:
- snapshots: bfloat16 [1024, 3, 32, 256], P(None, None, 'sx', 'sy'), may hold values from -6 to 6
- quad_weight: float32 [3, 32, 256], P(None, 'sx', 'sy'), may hold values from 0.5 to 1200
- mode_guess: float32 [16, 64, 2, 8], replicated, may hold values from -6 to 6
- bins: int32 [16], replicated, may hold values from 1 to 127
- starts: int32 [64], replicated, may hold values from 0 to 768
Outputs:
- modes: float32 [16, 2, 8, 3, 32, 256], P(None, None, None, None, 'sx', 'sy')
- energy: float32 [16, 8], replicated
The draws below stay inside these ranges and needn't reach their ends.
All inputs are finite; a program needn't handle non-finite values.
Results may differ from the reference program's by a relative error of at most 0.0024.
Values may be sent and summed in bfloat16 or wider, within the bound.
A program may use at most 64 MiB of HBM per device.

```python
import math
import jax
import jax.numpy as jnp
from jax import lax

NFFT = 256
NB = 64
NF = 16
NM = 8
TT = 1024
CX = 2
CY = 128
NSX = 32
NSY = 256


def draw_quad_weight(key, part):
    key_base = jax.random.fold_in(key, 11)
    key_tile = jax.random.fold_in(key, 12)
    key_heavy = jax.random.fold_in(key, 13)
    base = jnp.exp(jax.random.uniform(key_base, (3, NSX, NSY), jnp.float32, math.log(0.5), math.log(4.0)))
    tiles_x = NSX // CX
    tiles_y = NSY // CY
    ntiles = tiles_x * tiles_y
    tile_factor = jnp.exp(jax.random.uniform(key_tile, (ntiles,), jnp.float32, 0.0, math.log(10.0)))
    heavy = jax.random.permutation(key_heavy, ntiles)[:2]
    tile_factor = tile_factor.at[heavy].set(300.0)
    row_tile = jnp.arange(NSX, dtype=jnp.int32) // CX
    col_tile = jnp.arange(NSY, dtype=jnp.int32) // CY
    tile_ids = row_tile[:, None] * tiles_y + col_tile[None, :]
    factor = tile_factor[tile_ids]
    return base * factor[None]


def set_ends(values, own_key, low, largest):
    longest = values.shape.index(max(values.shape))
    spots = []
    for shift in (0, 1):
        where = [jax.random.randint(jax.random.fold_in(own_key, axis), (), 0, length) for axis, length in enumerate(values.shape)]
        where[longest] = (where[longest] + shift) % values.shape[longest]
        spots.append(tuple(where))
    return values.at[spots[0]].set(low).at[spots[1]].set(largest)


def levels(own_key, extent, split, low, high):
    level = 1.0
    for dim, blocks in split:
        steps = jax.random.uniform(jax.random.fold_in(jax.random.fold_in(own_key, 6), dim), (blocks,), jnp.float32, low / len(split), high / len(split))
        level = level * jnp.repeat(jnp.exp(steps), extent[dim] // blocks).reshape((-1,) + (1,) * (len(extent) - 1 - dim))
    return level


def scatter_about(stream_key, shape, deviation, most, cuts=(), held_as=jnp.bfloat16):
    drawn = deviation * jax.random.normal(stream_key, shape, jnp.float32)
    if cuts:
        drawn = drawn * levels(stream_key, shape, cuts, -0.22, 0.18)
    return jnp.clip(drawn, -most, most).astype(held_as)


def setup_inputs(seed: int = 0) -> dict:
    keys = jax.random.split(jax.random.key(seed), 6)
    snapshots = scatter_about(keys[0], (TT, 3, NSX, NSY), 1.0, 6.0, ((2, 16), (3, 2)))
    quad_weight = draw_quad_weight(jax.random.fold_in(keys[5], 71), 0)
    mode_guess = scatter_about(keys[2], (NF, NB, 2, NM), 1.0, 6.0, (), jnp.float32)
    bins = set_ends(jax.random.randint(keys[3], (NF,), 1, NFFT // 2), jax.random.fold_in(keys[3], 1), 1, (NFFT // 2) - 1).astype(jnp.int32)
    starts = set_ends(jax.random.randint(keys[4], (NB,), 0, TT - NFFT + 1), jax.random.fold_in(keys[4], 1), 0, TT - NFFT).astype(jnp.int32)
    return {"snapshots": snapshots, "quad_weight": quad_weight, "mode_guess": mode_guess, "bins": bins, "starts": starts}


EPS = 1e-06

def make_twiddle(bins):
    steps = jnp.arange(NFFT, dtype=jnp.int32)
    window = 0.5 - 0.5 * jnp.cos(2.0 * jnp.pi * steps.astype(jnp.float32) / NFFT)
    norm_c = 1.0 / jnp.sqrt(jnp.sum(window * window))
    phase = bins[:, None] * steps[None, :] % NFFT
    angle = 2.0 * jnp.pi * phase.astype(jnp.float32) / NFFT
    twid = jnp.stack([norm_c * window * jnp.cos(angle), -(norm_c * window) * jnp.sin(angle)], axis=1)
    return twid.astype(jnp.bfloat16)

def weighted_slice(snapshots, quad_weight, twid, scale, starts, index):
    piece = lax.dynamic_index_in_dim(snapshots, index, 2, keepdims=False)
    times = starts[:, None] + jnp.arange(NFFT, dtype=jnp.int32)[None, :]
    windows = jnp.take(piece, times, axis=0)
    qhat = jnp.einsum('fpt,btvy->fpbvy', twid.astype(jnp.float32), windows.astype(jnp.float32))
    wslice = lax.dynamic_index_in_dim(quad_weight, index, 1, keepdims=False)
    colscale = scale[:, None] * jnp.sqrt(wslice)
    ydata = (qhat * colscale[None, None, None]).astype(jnp.bfloat16)
    return ydata.reshape(NF, 2 * NB, 3 * NSY)

def reference(snapshots, quad_weight, mode_guess, bins, starts):
    twid = make_twiddle(bins)

    def square_step(total, index):
        piece = lax.dynamic_index_in_dim(snapshots, index, 2, keepdims=False).astype(jnp.float32)
        wslice = lax.dynamic_index_in_dim(quad_weight, index, 1, keepdims=False)
        return (total + lax.optimization_barrier(jnp.sum(piece * piece * wslice[None], axis=(0, 2))), None)
    sums, _ = lax.scan(square_step, jnp.zeros((3,), jnp.float32), jnp.arange(NSX, dtype=jnp.int32))
    msq = sums / (TT * NSX * NSY)
    scale = lax.rsqrt(msq + EPS)

    def gram_step(total, index):
        ydata = weighted_slice(snapshots, quad_weight, twid, scale, starts, index).astype(jnp.float32)
        return (total + jnp.einsum('fax,fbx->fab', ydata, ydata), None)
    gram, _ = lax.scan(gram_step, jnp.zeros((NF, 2 * NB, 2 * NB), jnp.float32), jnp.arange(NSX, dtype=jnp.int32))
    gram_re = gram[:, :NB, :NB] + gram[:, NB:, NB:]
    gram_im = gram[:, :NB, NB:] - gram[:, NB:, :NB]
    denom = 3.0 * NSX * NSY
    gram_re = gram_re / denom
    gram_im = gram_im / denom
    hp = lax.Precision.HIGHEST
    guess_re = mode_guess[:, :, 0, :]
    guess_im = mode_guess[:, :, 1, :]
    zre = jnp.einsum('fbc,fcn->fbn', gram_re, guess_re, precision=hp) - jnp.einsum('fbc,fcn->fbn', gram_im, guess_im, precision=hp)
    zim = jnp.einsum('fbc,fcn->fbn', gram_re, guess_im, precision=hp) + jnp.einsum('fbc,fcn->fbn', gram_im, guess_re, precision=hp)
    norms = lax.optimization_barrier(jnp.sum(zre * zre + zim * zim, axis=1))
    energy = jnp.sqrt(norms / NB)
    inv = lax.rsqrt(norms + EPS)[:, None, :]
    coef_re = (zre * inv).astype(jnp.bfloat16)
    coef_im = (zim * inv).astype(jnp.bfloat16)
    upper = jnp.concatenate([coef_re, coef_im], axis=-1)
    lower = jnp.concatenate([-coef_im, coef_re], axis=-1)
    stacked = jnp.concatenate([upper, lower], axis=1).astype(jnp.float32)

    def mode_step(index):
        ydata = weighted_slice(snapshots, quad_weight, twid, scale, starts, index).astype(jnp.float32)
        return jnp.einsum('fan,fax->fnx', stacked, ydata).reshape(NF, 2, NM, 3, NSY)
    slices = lax.map(mode_step, jnp.arange(NSX, dtype=jnp.int32))
    modes = jnp.transpose(slices, (1, 2, 3, 4, 0, 5))
    return (modes, energy)
```

```python
import functools
import math
import jax
import jax.numpy as jnp
from jax import lax
from jax.experimental import pallas as pl
from jax.experimental.pallas import tpu as pltpu
from jax.sharding import PartitionSpec as P

NFFT = 256
LANES = 128
EPS = 1e-06
MESH = pl.DeviceIdType.MESH


def horner(value, terms):
    total = terms[-1]
    for term in terms[-2::-1]:
        total = total * value + term
    return total


def turn(count):
    wrapped = jnp.where(count < NFFT // 2, count, count - NFFT)
    half = wrapped.astype(jnp.float32) * (math.pi / NFFT)
    sq = half * half
    sin = half * horner(sq, [(-1.0) ** k / math.factorial(2 * k + 1) for k in range(7)])
    cos = horner(sq, [(-1.0) ** k / math.factorial(2 * k) for k in range(8)])
    return 1.0 - 2.0 * sin * sin, 2.0 * sin * cos


def split(value):
    high = value.astype(jnp.bfloat16).astype(jnp.float32)
    return high, value - high


def fill_tables(bins, starts, nbins, nblock, nmode, cos_t, sin_t, cos_b, sin_b, wcat):
    lane = lax.broadcasted_iota(jnp.int32, (8, LANES), 1)
    sub = lax.broadcasted_iota(jnp.int32, (8, LANES), 0)
    row = jnp.zeros((8, LANES), jnp.int32)
    for b in range(nblock):
        row = jnp.where(lane == b, starts[b], row)
    for f in range(nbins):
        at = slice(f * nmode, (f + 1) * nmode)
        cos_b[at, :], sin_b[at, :] = turn(lax.rem(row * bins[f], NFFT))
    shape = (nbins, NFFT)
    which = lax.broadcasted_iota(jnp.int32, shape, 0)
    step = lax.broadcasted_iota(jnp.int32, shape, 1)
    number = jnp.zeros(shape, jnp.int32)
    for f in range(nbins):
        number = jnp.where(which == f, bins[f], number)
    cos, sin = turn(lax.rem(number * step, NFFT))
    for f in range(nbins):
        at = slice(f * nmode, (f + 1) * nmode)
        cos_t[at, :] = jnp.broadcast_to(cos[f:f + 1], (nmode, NFFT))
        sin_t[at, :] = jnp.broadcast_to(sin[f:f + 1], (nmode, NFFT))

    gain = 0.5 * math.sqrt(8.0 / (3.0 * NFFT))
    wave = [turn(lane + j * LANES) for j in range(NFFT // LANES)]
    length = wcat.shape[1]
    for g in range(nblock // 16):
        cols = []
        for h in range(2):
            col = jnp.zeros((8, LANES), jnp.int32)
            for i in range(8):
                col = jnp.where(sub == i, starts[g * 16 + h * 8 + i], col)
            cos_s, sin_s = turn(lax.rem(col, NFFT))
            cols.append((col, cos_s * gain, sin_s * gain))
        for j in range(length // LANES):
            ct, st = wave[j % (NFFT // LANES)]
            parts = []
            for col, cos_s, sin_s in cols:
                since = lane + j * LANES - col
                value = gain - (ct * cos_s + st * sin_s)
                parts.append(jnp.where((since >= 0) & (since < NFFT), value, 0.0))
            high, low = split(jnp.concatenate(parts, axis=0))
            high, low = high.astype(jnp.bfloat16), low.astype(jnp.bfloat16)
            at = slice(j * LANES, (j + 1) * LANES)
            for base, piece in ((0, high), (1, high), (2, low), (3, low)):
                wcat[base * nblock + g * 16:base * nblock + g * 16 + 16, at] = piece


def spread_over_time(nbins, nmode, lhs, wcat, cos_t, sin_t, a_ref):
    both = jnp.concatenate([lhs[...], lhs[...]], axis=1)
    for j in range(wcat.shape[1] // NFFT):
        at = slice(j * NFFT, (j + 1) * NFFT)
        b = jnp.dot(both, wcat[:, at], preferred_element_type=jnp.float32)
        for f in range(nbins):
            rows = slice(f * nmode, (f + 1) * nmode)
            c, s = cos_t[rows, :], sin_t[rows, :]
            re = b[2 * f * nmode:(2 * f + 1) * nmode]
            im = b[(2 * f + 1) * nmode:(2 * f + 2) * nmode]
            a_ref[2 * f * nmode:(2 * f + 2) * nmode, at] = jnp.concatenate(
                [c * re + s * im, c * im - s * re], axis=0
            ).astype(jnp.bfloat16)


def main_kernel(dims, starts_hbm, bins_hbm, x_hbm, quad_hbm, guess_hbm,
                z_ref, xr, wcat, cos_t, sin_t, cols_ref,
                starts, bins, x_ref, quad_ref, guess_ref, xs, cos_b, sin_b, lhs, a_ref,
                sq, sqbuf, zsend, zrecv, zall, load_sems, sems):
    (length, nvar, ctile, nblock, nbins, nmode, n_x, n_y, per, grid_points) = dims
    n = n_x * n_y
    me = lax.axis_index("sx") * n_y + lax.axis_index("sy")
    per_var = ctile // nvar
    loads = [
        pltpu.make_async_copy(src, dst, load_sems.at[i])
        for i, (src, dst) in enumerate(
            [
                (bins_hbm, bins),
                (starts_hbm, starts),
                (guess_hbm, guess_ref),
                (quad_hbm, quad_ref),
                (x_hbm, x_ref),
            ]
        )
    ]
    for load in loads:
        load.start()

    ix, iy = lax.axis_index("sx"), lax.axis_index("sy")

    def each_partner(act):
        def pick(dx, dy):
            tx, ty = lax.rem(ix + dx, n_x), lax.rem(iy + dy, n_y)
            act(tx * n_y + ty, (tx, ty))

        for dy in range(1, n_y):
            pick(0, dy)

        def go(dx, carry):
            for dy in range(n_y):
                pick(dx, dy)
            return carry

        lax.fori_loop(1, n_x, go, 0, unroll=5)

    barrier = pltpu.get_barrier_semaphore()
    each_partner(
        lambda t, where: pl.semaphore_signal(
            barrier, inc=1, device_id=where, device_id_type=MESH
        )
    )

    def spread(src, dst, phase, by_target):
        each_partner(
            lambda t, where: pltpu.make_async_remote_copy(
                src_ref=src.at[t] if by_target else src,
                dst_ref=dst.at[me],
                send_sem=sems.at[2 * phase],
                recv_sem=sems.at[2 * phase + 1],
                device_id=where,
                device_id_type=MESH,
            ).start()
        )

    def wait_all(dst, sem):
        rest = dst.at[pl.ds(0, n - 1)]
        pltpu.make_async_copy(rest, rest, sems.at[sem]).wait()

    with jax.named_scope("tables"):
        loads[0].wait()
        loads[1].wait()
        fill_tables(bins, starts, nbins, nblock, nmode, cos_t, sin_t, cos_b, sin_b, wcat)
    with jax.named_scope("guess"):
        loads[2].wait()
        for f in range(nbins):
            rows = slice(f * nmode, (f + 1) * nmode)
            c, s = cos_b[rows, :nblock], sin_b[rows, :nblock]
            g_re, g_im = guess_ref[f, 0], guess_ref[f, 1]
            value = jnp.concatenate([g_re * c - g_im * s, g_re * s + g_im * c], axis=0)
            high, low = split(value)
            lhs[2 * f * nmode:(2 * f + 2) * nmode, :] = jnp.concatenate(
                [high, low], axis=1
            ).astype(jnp.bfloat16)
    with jax.named_scope("acoef"):
        spread_over_time(nbins, nmode, lhs, wcat, cos_t, sin_t, a_ref)
    with jax.named_scope("loadwait"):
        loads[3].wait()
        loads[4].wait()
    rows = x_ref.shape[0]
    step = rows // 16

    with jax.named_scope("conv"):
        @pl.loop(0, 16)
        def _(i):
            at = pl.ds(pl.multiple_of(i * step, step), step)
            xs[at, :] = x_ref[at, :].astype(jnp.float32)

    lane = lax.broadcasted_iota(jnp.int32, (1, LANES), 1)
    with jax.named_scope("squares"):
        quads = [quad_ref[c // per_var, c % per_var:c % per_var + 1, :] for c in range(ctile)]
        total = jnp.zeros((1, LANES), jnp.float32)
        for c in range(ctile):
            col = xs[pl.ds(c, length, stride=ctile), :]
            xr[:, c * LANES:(c + 1) * LANES] = col.astype(jnp.bfloat16)
            sums = jnp.sum(col * col, axis=0, keepdims=True) * quads[c]
            one = jnp.sum(sums, axis=1, keepdims=True)
            total = total + jnp.where(lane == c // per_var, one, 0.0)
        sq[...] = total

    low_half = lax.broadcasted_iota(jnp.int32, (nmode, LANES), 1) < nblock
    parts = nmode // per
    span = per_var * LANES
    for v in range(nvar):
        with jax.named_scope(f"var{v}"):
            at = slice(v * span, (v + 1) * span)
            weight = jnp.concatenate(quads[v * per_var:(v + 1) * per_var], axis=1)
            u = jnp.dot(a_ref[...], xr[:, at], preferred_element_type=jnp.float32)
            u = (u * weight).astype(jnp.bfloat16)
            acc = None
            for j in range(length // NFFT):
                steps = slice(j * NFFT, (j + 1) * NFFT)
                back = lax.dot_general(
                    u, xr[steps, at], (((1,), (1,)), ((), ())),
                    preferred_element_type=jnp.float32,
                )
                turned = []
                for f in range(nbins):
                    rows = slice(f * nmode, (f + 1) * nmode)
                    c, s = cos_t[rows, :], sin_t[rows, :]
                    re = back[2 * f * nmode:(2 * f + 1) * nmode]
                    im = back[(2 * f + 1) * nmode:(2 * f + 2) * nmode]
                    turned.append(
                        jnp.concatenate([c * re - s * im, s * re + c * im], axis=0).astype(
                            jnp.bfloat16
                        )
                    )
                one = lax.dot_general(
                    jnp.concatenate(turned, axis=0), wcat[nblock:3 * nblock, steps],
                    (((1,), (1,)), ((), ())), preferred_element_type=jnp.float32,
                )
                acc = one if acc is None else acc + one
            acc = (acc + pltpu.roll(acc, nblock, 1)) * (1.0 / (3.0 * grid_points))
            for f in range(nbins):
                z = jnp.where(
                    low_half,
                    acc[2 * f * nmode:(2 * f + 1) * nmode],
                    acc[(2 * f + 1) * nmode:(2 * f + 2) * nmode],
                )
                for s in range(parts):
                    zsend[f * parts + s, v] = z[s * per:(s + 1) * per]
    owners = nbins * parts
    for s in range(owners, n):
        zsend[s] = jnp.zeros((nvar, per, LANES), jnp.float32)

    with jax.named_scope("barrier"):
        pl.semaphore_wait(barrier, n - 1)
    with jax.named_scope("send"):
        spread(sq, sqbuf, 0, False)
        spread(zsend, zrecv, 1, True)
    with jax.named_scope("sqwait"):
        wait_all(sqbuf, 1)
        sqbuf[me] = sq[...]
        total = jnp.sum(sqbuf[...], axis=0)
        scale = lax.rsqrt(total / (length * grid_points) + EPS)
        scales = [
            jnp.sum(jnp.where(lane == v, scale, 0.0), axis=1, keepdims=True) for v in range(nvar)
        ]
        for c in range(ctile):
            cols_ref[c:c + 1, :] = scales[c // per_var] * jnp.sqrt(quads[c])
    with jax.named_scope("a2a"):
        wait_all(zrecv, 3)
    with jax.named_scope("zsum"):
        zrecv[me] = zsend[me]
        sums = jnp.sum(zrecv[...], axis=0)
        z = sums[0] * (scales[0] * scales[0])
        for v in range(1, nvar):
            z = z + sums[v] * (scales[v] * scales[v])
        zall[me] = z
    with jax.named_scope("ag"):
        spread(zall.at[me], zall, 2, False)
        wait_all(zall, 5)
    for s in range(owners):
        z_ref[s * per:(s + 1) * per] = zall[s]
    wait_all(zrecv, 2)
    wait_all(zall, 4)
    wait_all(sqbuf, 0)


def modes_kernel(dims, z_ref, xr, wcat, cos_t, sin_t, cols_ref, modes_hbm, energy_ref,
                 lhs, a_ref, out, sems):
    nvar, ctile, nblock, nbins, nmode = dims
    low_half = lax.broadcasted_iota(jnp.int32, (nmode, LANES), 1) < nblock
    column = lax.broadcasted_iota(jnp.int32, (nmode, nbins), 1)
    energy = jnp.zeros((nmode, nbins), jnp.float32)
    for f in range(nbins):
        z = z_ref[f * nmode:(f + 1) * nmode]
        norms = jnp.sum(z * z, axis=1, keepdims=True)
        energy = jnp.where(column == f, jnp.sqrt(norms / nblock), energy)
        high, low = split(z * lax.rsqrt(norms + EPS))
        lhs[2 * f * nmode:(2 * f + 2) * nmode, :] = jnp.concatenate(
            [
                jnp.where(low_half, high, pltpu.roll(low, nblock, 1)),
                jnp.where(low_half, pltpu.roll(high, nblock, 1), low),
            ],
            axis=0,
        ).astype(jnp.bfloat16)
    energy_ref[...] = energy
    with jax.named_scope("macoef"):
        spread_over_time(nbins, nmode, lhs, wcat, cos_t, sin_t, a_ref)
    per_var = ctile // nvar
    span = per_var * LANES
    rows = 2 * nbins * nmode
    with jax.named_scope("mdot"):
        for v in range(nvar):
            m = jnp.dot(
                a_ref[...], xr[:, v * span:(v + 1) * span], preferred_element_type=jnp.float32
            )
            for k in range(per_var):
                c = v * per_var + k
                out[pl.ds(c, rows, stride=ctile), :] = (
                    m[:, k * LANES:(k + 1) * LANES] * cols_ref[c:c + 1, :]
                )
    with jax.named_scope("mout"):
        copy = pltpu.make_async_copy(out, modes_hbm, sems.at[0])
        copy.start()
        copy.wait()


def shards(n_x, n_y, snapshots, quad_weight, mode_guess, bins, starts):
    length, nvar, cols_x, cols_y = snapshots.shape
    nbins = bins.shape[0]
    nblock = starts.shape[0]
    nmode = mode_guess.shape[-1]
    ctile = nvar * cols_x
    points = ctile * cols_y
    n = n_x * n_y
    grid_points = cols_x * cols_y * n
    vmem = pl.BlockSpec(memory_space=pltpu.VMEM)
    hbm = pl.BlockSpec(memory_space=pltpu.HBM)
    limit = 30 * 1024 * 1024
    rows = 2 * nbins * nmode

    x = snapshots.reshape(length * ctile, cols_y)
    guess = jnp.transpose(mode_guess, (0, 2, 3, 1))

    operands = [
        pltpu.with_memory_space_constraint(value, pltpu.HBM)
        for value in (starts, bins, x, quad_weight, guess)
    ]
    per = max(1, nbins * nmode // n)
    dims = (length, nvar, ctile, nblock, nbins, nmode, n_x, n_y, per, grid_points)
    z, *kept = pl.pallas_call(
        functools.partial(main_kernel, dims),
        name="spod",
        out_shape=(
            jax.ShapeDtypeStruct((nbins * nmode, LANES), jnp.float32),
            jax.ShapeDtypeStruct((length, points), jnp.bfloat16),
            jax.ShapeDtypeStruct((4 * nblock, length), jnp.bfloat16),
            jax.ShapeDtypeStruct((nbins * nmode, NFFT), jnp.float32),
            jax.ShapeDtypeStruct((nbins * nmode, NFFT), jnp.float32),
            jax.ShapeDtypeStruct((8, LANES), jnp.float32),
        ),
        in_specs=[hbm] * 5,
        out_specs=(vmem,) * 6,
        scratch_shapes=[
            pltpu.SMEM(starts.shape, jnp.int32),
            pltpu.SMEM(bins.shape, jnp.int32),
            pltpu.VMEM(x.shape, jnp.bfloat16),
            pltpu.VMEM(quad_weight.shape, jnp.float32),
            pltpu.VMEM(guess.shape, jnp.float32),
            pltpu.VMEM((length * ctile, cols_y), jnp.float32),
            pltpu.VMEM((nbins * nmode, LANES), jnp.float32),
            pltpu.VMEM((nbins * nmode, LANES), jnp.float32),
            pltpu.VMEM((rows, 2 * nblock), jnp.bfloat16),
            pltpu.VMEM((rows, length), jnp.bfloat16),
            pltpu.VMEM((1, LANES), jnp.float32),
            pltpu.VMEM((n, 1, LANES), jnp.float32),
            pltpu.VMEM((n, nvar, per, LANES), jnp.float32),
            pltpu.VMEM((n, nvar, per, LANES), jnp.float32),
            pltpu.VMEM((n, per, LANES), jnp.float32),
            pltpu.SemaphoreType.DMA((5,)),
            pltpu.SemaphoreType.DMA((6,)),
        ],
        compiler_params=pltpu.CompilerParams(
            collective_id=0, has_side_effects=True, vmem_limit_bytes=limit
        ),
    )(*operands)

    modes, energy = pl.pallas_call(
        functools.partial(modes_kernel, (nvar, ctile, nblock, nbins, nmode)),
        name="modes",
        out_shape=(
            jax.ShapeDtypeStruct((rows * ctile, cols_y), jnp.float32),
            jax.ShapeDtypeStruct((nmode, nbins), jnp.float32),
        ),
        in_specs=[vmem] * 6,
        out_specs=(hbm, vmem),
        scratch_shapes=[
            pltpu.VMEM((rows, 2 * nblock), jnp.bfloat16),
            pltpu.VMEM((rows, length), jnp.bfloat16),
            pltpu.VMEM((rows * ctile, cols_y), jnp.float32),
            pltpu.SemaphoreType.DMA((1,)),
        ],
        compiler_params=pltpu.CompilerParams(vmem_limit_bytes=limit),
    )(z, *kept)
    return (
        modes.reshape(nbins, 2, nmode, nvar, cols_x, cols_y),
        energy.T,
    )


def solution(mesh):
    n_x, n_y = mesh.shape["sx"], mesh.shape["sy"]
    return jax.shard_map(
        functools.partial(shards, n_x, n_y),
        mesh=mesh,
        in_specs=(P(None, None, "sx", "sy"), P(None, "sx", "sy"), P(), P(), P()),
        out_specs=(P(None, None, None, None, "sx", "sy"), P()),
        check_vma=False,
    )
```

```python
import functools
import math
import jax
import jax.numpy as jnp
from jax import lax
from jax.experimental import pallas as pl
from jax.experimental.pallas import tpu as pltpu
from jax.sharding import PartitionSpec as P

NFFT = 256
LANES = 128
EPS = 1e-06
MESH = pl.DeviceIdType.MESH


def horner(value, terms):
    total = terms[-1]
    for term in terms[-2::-1]:
        total = total * value + term
    return total


def turn(count):
    wrapped = jnp.where(count < NFFT // 2, count, count - NFFT)
    half = wrapped.astype(jnp.float32) * (math.pi / NFFT)
    sq = half * half
    sin = half * horner(sq, [(-1.0) ** k / math.factorial(2 * k + 1) for k in range(7)])
    cos = horner(sq, [(-1.0) ** k / math.factorial(2 * k) for k in range(8)])
    return 1.0 - 2.0 * sin * sin, 2.0 * sin * cos


def split(value):
    high = value.astype(jnp.bfloat16).astype(jnp.float32)
    return high, value - high


def fill_tables(bins, starts, nbins, nblock, nmode, cos_t, sin_t, cos_b, sin_b, wcat):
    lane = lax.broadcasted_iota(jnp.int32, (8, LANES), 1)
    sub = lax.broadcasted_iota(jnp.int32, (8, LANES), 0)
    row = jnp.zeros((8, LANES), jnp.int32)
    for b in range(nblock):
        row = jnp.where(lane == b, starts[b], row)
    for f in range(nbins):
        at = slice(f * nmode, (f + 1) * nmode)
        cos_b[at, :], sin_b[at, :] = turn(lax.rem(row * bins[f], NFFT))
    shape = (nbins, NFFT)
    which = lax.broadcasted_iota(jnp.int32, shape, 0)
    step = lax.broadcasted_iota(jnp.int32, shape, 1)
    number = jnp.zeros(shape, jnp.int32)
    for f in range(nbins):
        number = jnp.where(which == f, bins[f], number)
    cos, sin = turn(lax.rem(number * step, NFFT))
    for f in range(nbins):
        at = slice(f * nmode, (f + 1) * nmode)
        cos_t[at, :] = jnp.broadcast_to(cos[f:f + 1], (nmode, NFFT))
        sin_t[at, :] = jnp.broadcast_to(sin[f:f + 1], (nmode, NFFT))

    gain = 0.5 * math.sqrt(8.0 / (3.0 * NFFT))
    wave = [turn(lane + j * LANES) for j in range(NFFT // LANES)]
    length = wcat.shape[1]
    for g in range(nblock // 16):
        cols = []
        for h in range(2):
            col = jnp.zeros((8, LANES), jnp.int32)
            for i in range(8):
                col = jnp.where(sub == i, starts[g * 16 + h * 8 + i], col)
            cos_s, sin_s = turn(lax.rem(col, NFFT))
            cols.append((col, cos_s * gain, sin_s * gain))
        for j in range(length // LANES):
            ct, st = wave[j % (NFFT // LANES)]
            parts = []
            for col, cos_s, sin_s in cols:
                since = lane + j * LANES - col
                value = gain - (ct * cos_s + st * sin_s)
                parts.append(jnp.where((since >= 0) & (since < NFFT), value, 0.0))
            high, low = split(jnp.concatenate(parts, axis=0))
            high, low = high.astype(jnp.bfloat16), low.astype(jnp.bfloat16)
            at = slice(j * LANES, (j + 1) * LANES)
            for base, piece in ((0, high), (1, high), (2, low), (3, low)):
                wcat[base * nblock + g * 16:base * nblock + g * 16 + 16, at] = piece


def rotate_windows(nbins, nmode, lhs, rhs, cos_t, sin_t, store):
    for j in range(rhs.shape[1] // NFFT):
        at = slice(j * NFFT, (j + 1) * NFFT)
        b = jnp.dot(lhs, rhs[:, at], preferred_element_type=jnp.float32)
        for f in range(nbins):
            rows = slice(f * nmode, (f + 1) * nmode)
            c, s = cos_t[rows, :], sin_t[rows, :]
            re = b[2 * f * nmode:(2 * f + 1) * nmode]
            im = b[(2 * f + 1) * nmode:(2 * f + 2) * nmode]
            store(
                slice(2 * f * nmode, (2 * f + 2) * nmode),
                j,
                jnp.concatenate([c * re + s * im, c * im - s * re], axis=0),
            )


def three(value):
    high, rest = split(value)
    mid, low = split(rest)
    return high, mid, low


def main_kernel(dims, starts_hbm, bins_hbm, x_hbm, quad_hbm, guess_hbm,
                gall, xr, wcat, cos_t, sin_t, roots_ref,
                starts, bins, x_ref, quad_ref, guess_ref, xs, cos_b, sin_b, lhs, a_ref,
                zsend, zrecv, load_sems, sems):
    (length, nvar, ctile, nblock, nbins, nmode, n_x, n_y, first, grid_points) = dims
    n = n_x * n_y
    me = lax.axis_index("sx") * n_y + lax.axis_index("sy")
    slot = me - first
    owner = jnp.logical_and(slot >= 0, slot < nbins)
    per_var = ctile // nvar
    loads = [
        pltpu.make_async_copy(src, dst, load_sems.at[i])
        for i, (src, dst) in enumerate(
            [
                (bins_hbm, bins),
                (starts_hbm, starts),
                (guess_hbm, guess_ref),
                (quad_hbm, quad_ref),
                (x_hbm, x_ref),
            ]
        )
    ]
    for load in loads:
        load.start()

    def each_owner(act):
        @pl.loop(0, nbins, unroll=4)
        def _(k):
            to = lax.rem(me + k, nbins)
            where = first + to

            @pl.when(where != me)
            def _():
                act(to, (where // n_y, lax.rem(where, n_y)))

    def each_other(act):
        @pl.loop(1, n, unroll=4)
        def _(k):
            where = lax.rem(me + k, n)
            act((where // n_y, lax.rem(where, n_y)))

    barrier = pltpu.get_barrier_semaphore()

    def greet(where):
        pl.semaphore_signal(barrier, inc=1, device_id=where, device_id_type=MESH)

    @pl.when(owner)
    def _():
        each_other(greet)

    @pl.when(jnp.logical_not(owner))
    def _():
        each_owner(lambda to, where: greet(where))

    with jax.named_scope("tables"):
        loads[0].wait()
        loads[1].wait()
        fill_tables(bins, starts, nbins, nblock, nmode, cos_t, sin_t, cos_b, sin_b, wcat)
    with jax.named_scope("guess"):
        loads[2].wait()
        for f in range(nbins):
            rows = slice(f * nmode, (f + 1) * nmode)
            c, s = cos_b[rows, :nblock], sin_b[rows, :nblock]
            g_re, g_im = guess_ref[f, 0], guess_ref[f, 1]
            value = jnp.concatenate([g_re * c - g_im * s, g_re * s + g_im * c], axis=0)
            high, low = split(value)
            lhs[2 * f * nmode:(2 * f + 2) * nmode, :] = jnp.concatenate(
                [high, low], axis=1
            ).astype(jnp.bfloat16)
    with jax.named_scope("acoef"):
        def keep(rows, j, value):
            a_ref[rows, j * NFFT:(j + 1) * NFFT] = value.astype(jnp.bfloat16)

        rotate_windows(
            nbins, nmode, jnp.concatenate([lhs[...], lhs[...]], axis=1), wcat, cos_t, sin_t, keep
        )
    with jax.named_scope("loadwait"):
        loads[3].wait()
        loads[4].wait()
    rows = x_ref.shape[0]
    step = rows // 16

    with jax.named_scope("conv"):
        @pl.loop(0, 16)
        def _(i):
            at = pl.ds(pl.multiple_of(i * step, step), step)
            xs[at, :] = x_ref[at, :].astype(jnp.float32)

    lane = lax.broadcasted_iota(jnp.int32, (1, LANES), 1)
    with jax.named_scope("squares"):
        quads = [quad_ref[c // per_var, c % per_var:c % per_var + 1, :] for c in range(ctile)]
        total = jnp.zeros((1, LANES), jnp.float32)
        for c in range(ctile):
            roots_ref[c:c + 1, :] = jnp.sqrt(quads[c])
            col = xs[pl.ds(c, length, stride=ctile), :]
            xr[:, c * LANES:(c + 1) * LANES] = col.astype(jnp.bfloat16)
            sums = jnp.sum(col * col, axis=0, keepdims=True) * quads[c]
            one = jnp.sum(sums, axis=1, keepdims=True)
            total = total + jnp.where(lane == c // per_var, one, 0.0)

    low_half = lax.broadcasted_iota(jnp.int32, (nmode, LANES), 1) < nblock
    sub = lax.broadcasted_iota(jnp.int32, (nmode, LANES), 0)
    span = per_var * LANES
    folded = []
    for v in range(nvar):
        with jax.named_scope(f"var{v}"):
            at = slice(v * span, (v + 1) * span)
            weight = jnp.concatenate(quads[v * per_var:(v + 1) * per_var], axis=1)
            u = jnp.dot(a_ref[...], xr[:, at], preferred_element_type=jnp.float32)
            u = (u * weight).astype(jnp.bfloat16)
            acc = None
            for j in range(length // NFFT):
                steps = slice(j * NFFT, (j + 1) * NFFT)
                back = lax.dot_general(
                    u, xr[steps, at], (((1,), (1,)), ((), ())),
                    preferred_element_type=jnp.float32,
                )
                turned = []
                for f in range(nbins):
                    rows = slice(f * nmode, (f + 1) * nmode)
                    c, s = cos_t[rows, :], sin_t[rows, :]
                    re = back[2 * f * nmode:(2 * f + 1) * nmode]
                    im = back[(2 * f + 1) * nmode:(2 * f + 2) * nmode]
                    turned.append(
                        jnp.concatenate([c * re - s * im, s * re + c * im], axis=0).astype(
                            jnp.bfloat16
                        )
                    )
                one = lax.dot_general(
                    jnp.concatenate(turned, axis=0), wcat[nblock:3 * nblock, steps],
                    (((1,), (1,)), ((), ())), preferred_element_type=jnp.float32,
                )
                acc = one if acc is None else acc + one
            folded.append((acc + pltpu.roll(acc, nblock, 1)) * (1.0 / (3.0 * grid_points)))
    with jax.named_scope("pack"):
        pieces = jnp.zeros((nmode, LANES), jnp.float32)
        for i, piece in enumerate(three(total)):
            pieces = jnp.where(sub == i, piece, pieces)
        for f in range(nbins):
            re = slice(2 * f * nmode, (2 * f + 1) * nmode)
            im = slice((2 * f + 1) * nmode, (2 * f + 2) * nmode)
            zsend[f] = jnp.concatenate(
                [jnp.where(low_half, one[re], one[im]) for one in folded] + [pieces], axis=0
            ).astype(jnp.bfloat16)

    with jax.named_scope("barrier"):
        pl.semaphore_wait(barrier, jnp.where(owner, n - 1, nbins))
    with jax.named_scope("send"):
        each_owner(
            lambda to, where: pltpu.make_async_remote_copy(
                src_ref=zsend.at[to],
                dst_ref=zrecv.at[me],
                send_sem=sems.at[0],
                recv_sem=sems.at[1],
                device_id=where,
                device_id_type=MESH,
            ).start()
        )

    def wait_for(ref, sem):
        pltpu.make_async_copy(ref, ref, sems.at[sem]).wait()

    @pl.when(owner)
    def _():
        with jax.named_scope("a2a"):
            wait_for(zrecv.at[pl.ds(0, n - 1)], 1)
        with jax.named_scope("zsum"):
            zrecv[me] = zsend[slot]
            sums = jnp.sum(zrecv[...].astype(jnp.float32), axis=0)
            total = jnp.sum(sums[nvar * nmode:], axis=0, keepdims=True)
            scale = lax.rsqrt(total / (length * grid_points) + EPS)
            square = scale * scale
            z = jnp.zeros((nmode, LANES), jnp.float32)
            for v in range(nvar):
                factor = jnp.sum(jnp.where(lane == v, square, 0.0), axis=1, keepdims=True)
                z = z + sums[v * nmode:(v + 1) * nmode] * factor
            norms = jnp.sum(z * z, axis=1, keepdims=True)
            energy = jnp.sqrt(norms / nblock)
            wide = lax.broadcasted_iota(jnp.int32, (nmode, LANES), 1)
            extra = jnp.zeros((nmode, LANES), jnp.float32)
            for i, piece in enumerate(three(energy)):
                extra = jnp.where(wide == i, piece, extra)
            for i, piece in enumerate(three(scale)):
                moved = pltpu.roll(
                    jnp.broadcast_to(piece, (nmode, LANES)), 3 + i * nvar, 1
                )
                inside = jnp.logical_and(wide >= 3 + i * nvar, wide < 3 + (i + 1) * nvar)
                extra = jnp.where(inside, moved, extra)
            gall[slot] = jnp.concatenate([z * lax.rsqrt(norms + EPS), extra], axis=0).astype(
                jnp.bfloat16
            )
        with jax.named_scope("agsend"):
            each_other(
                lambda where: pltpu.make_async_remote_copy(
                    src_ref=gall.at[slot],
                    dst_ref=gall.at[slot],
                    send_sem=sems.at[2],
                    recv_sem=sems.at[3],
                    device_id=where,
                    device_id_type=MESH,
                ).start()
            )
        with jax.named_scope("ag"):
            wait_for(gall.at[pl.ds(0, nbins - 1)], 3)
            wait_for(zsend.at[pl.ds(0, nbins - 1)], 0)
            for _ in range((n - 1) // (nbins - 1)):
                wait_for(gall.at[pl.ds(0, nbins - 1)], 2)
            rest = (n - 1) % (nbins - 1)
            if rest:
                wait_for(gall.at[pl.ds(0, rest)], 2)

    @pl.when(jnp.logical_not(owner))
    def _():
        with jax.named_scope("ag"):
            wait_for(gall, 3)
            wait_for(zsend, 0)


def modes_kernel(dims, gall, xr, wcat, cos_t, sin_t, roots_ref, modes_hbm, energy_ref,
                 a_ref, out, sems):
    length, nvar, ctile, nblock, nbins, nmode = dims
    low_half = lax.broadcasted_iota(jnp.int32, (nmode, LANES), 1) < nblock
    lane = lax.broadcasted_iota(jnp.int32, (nmode, LANES), 1)
    column = lax.broadcasted_iota(jnp.int32, (nmode, nbins), 1)
    energy = jnp.zeros((nmode, nbins), jnp.float32)
    lhs = []
    for f in range(nbins):
        message = gall[f].astype(jnp.float32)
        coef, extra = message[:nmode], message[nmode:]
        one = jnp.sum(jnp.where(lane < 3, extra, 0.0), axis=1, keepdims=True)
        energy = jnp.where(column == f, one, energy)
        swapped = pltpu.roll(coef, nblock, 1)
        lhs.append(
            jnp.concatenate(
                [jnp.where(low_half, coef, swapped), jnp.where(low_half, swapped, coef)], axis=0
            ).astype(jnp.bfloat16)
        )
    energy_ref[...] = energy
    extra = gall[0].astype(jnp.float32)[nmode:nmode + 1]
    scales = []
    for v in range(nvar):
        mine = jnp.zeros((1, LANES), jnp.bool_)
        for i in range(3):
            mine = jnp.logical_or(mine, lane[:1] == 3 + i * nvar + v)
        scales.append(jnp.sum(jnp.where(mine, extra, 0.0), axis=1, keepdims=True))
    with jax.named_scope("macoef"):
        def keep(rows, j, value):
            high, low = split(value)
            a_ref[rows, j * NFFT:(j + 1) * NFFT] = high.astype(jnp.bfloat16)
            a_ref[rows, length + j * NFFT:length + (j + 1) * NFFT] = low.astype(jnp.bfloat16)

        rotate_windows(
            nbins, nmode, jnp.concatenate(lhs, axis=0), wcat.at[nblock:3 * nblock],
            cos_t, sin_t, keep
        )
    per_var = ctile // nvar
    span = per_var * LANES
    rows = 2 * nbins * nmode
    with jax.named_scope("mdot"):
        for v in range(nvar):
            at = slice(v * span, (v + 1) * span)
            m = jnp.dot(a_ref[:, :length], xr[:, at], preferred_element_type=jnp.float32)
            m = m + jnp.dot(a_ref[:, length:], xr[:, at], preferred_element_type=jnp.float32)
            for k in range(per_var):
                c = v * per_var + k
                out[pl.ds(c, rows, stride=ctile), :] = m[:, k * LANES:(k + 1) * LANES] * (
                    scales[v] * roots_ref[c:c + 1, :]
                )
    with jax.named_scope("mout"):
        copy = pltpu.make_async_copy(out, modes_hbm, sems.at[0])
        copy.start()
        copy.wait()


def shards(n_x, n_y, snapshots, quad_weight, mode_guess, bins, starts):
    length, nvar, cols_x, cols_y = snapshots.shape
    nbins = bins.shape[0]
    nblock = starts.shape[0]
    nmode = mode_guess.shape[-1]
    ctile = nvar * cols_x
    points = ctile * cols_y
    n = n_x * n_y
    grid_points = cols_x * cols_y * n
    vmem = pl.BlockSpec(memory_space=pltpu.VMEM)
    hbm = pl.BlockSpec(memory_space=pltpu.HBM)
    limit = 30 * 1024 * 1024
    rows = 2 * nbins * nmode

    x = snapshots.reshape(length * ctile, cols_y)
    guess = jnp.transpose(mode_guess, (0, 2, 3, 1))

    operands = [
        pltpu.with_memory_space_constraint(value, pltpu.HBM)
        for value in (starts, bins, x, quad_weight, guess)
    ]
    first = (n - nbins) // 2
    dims = (length, nvar, ctile, nblock, nbins, nmode, n_x, n_y, first, grid_points)
    gall, *kept = pl.pallas_call(
        functools.partial(main_kernel, dims),
        name="spod",
        out_shape=(
            jax.ShapeDtypeStruct((nbins, 2 * nmode, LANES), jnp.bfloat16),
            jax.ShapeDtypeStruct((length, points), jnp.bfloat16),
            jax.ShapeDtypeStruct((4 * nblock, length), jnp.bfloat16),
            jax.ShapeDtypeStruct((nbins * nmode, NFFT), jnp.float32),
            jax.ShapeDtypeStruct((nbins * nmode, NFFT), jnp.float32),
            jax.ShapeDtypeStruct((8, LANES), jnp.float32),
        ),
        in_specs=[hbm] * 5,
        out_specs=(vmem,) * 6,
        scratch_shapes=[
            pltpu.SMEM(starts.shape, jnp.int32),
            pltpu.SMEM(bins.shape, jnp.int32),
            pltpu.VMEM(x.shape, jnp.bfloat16),
            pltpu.VMEM(quad_weight.shape, jnp.float32),
            pltpu.VMEM(guess.shape, jnp.float32),
            pltpu.VMEM((length * ctile, cols_y), jnp.float32),
            pltpu.VMEM((nbins * nmode, LANES), jnp.float32),
            pltpu.VMEM((nbins * nmode, LANES), jnp.float32),
            pltpu.VMEM((rows, 2 * nblock), jnp.bfloat16),
            pltpu.VMEM((rows, length), jnp.bfloat16),
            pltpu.VMEM((nbins, (nvar + 1) * nmode, LANES), jnp.bfloat16),
            pltpu.VMEM((n, (nvar + 1) * nmode, LANES), jnp.bfloat16),
            pltpu.SemaphoreType.DMA((5,)),
            pltpu.SemaphoreType.DMA((4,)),
        ],
        compiler_params=pltpu.CompilerParams(
            collective_id=0, has_side_effects=True, vmem_limit_bytes=limit
        ),
    )(*operands)

    modes, energy = pl.pallas_call(
        functools.partial(modes_kernel, (length, nvar, ctile, nblock, nbins, nmode)),
        name="modes",
        out_shape=(
            jax.ShapeDtypeStruct((rows * ctile, cols_y), jnp.float32),
            jax.ShapeDtypeStruct((nmode, nbins), jnp.float32),
        ),
        in_specs=[vmem] * 6,
        out_specs=(hbm, vmem),
        scratch_shapes=[
            pltpu.VMEM((rows, 2 * length), jnp.bfloat16),
            pltpu.VMEM((rows * ctile, cols_y), jnp.float32),
            pltpu.SemaphoreType.DMA((1,)),
        ],
        compiler_params=pltpu.CompilerParams(vmem_limit_bytes=limit),
    )(gall, *kept)
    return (
        modes.reshape(nbins, 2, nmode, nvar, cols_x, cols_y),
        energy.T,
    )


def solution(mesh):
    n_x, n_y = mesh.shape["sx"], mesh.shape["sy"]
    return jax.shard_map(
        functools.partial(shards, n_x, n_y),
        mesh=mesh,
        in_specs=(P(None, None, "sx", "sy"), P(None, "sx", "sy"), P(), P(), P()),
        out_specs=(P(None, None, None, None, "sx", "sy"), P()),
        check_vma=False,
    )
```

```python
import functools
import math
import jax
import jax.numpy as jnp
from jax import lax
from jax.experimental import pallas as pl
from jax.experimental.pallas import tpu as pltpu
from jax.sharding import PartitionSpec as P

NFFT = 256
LANES = 128
EPS = 1e-06
MESH = pl.DeviceIdType.MESH


def horner(value, terms):
    total = terms[-1]
    for term in terms[-2::-1]:
        total = total * value + term
    return total


def turn(count):
    wrapped = jnp.where(count < NFFT // 2, count, count - NFFT)
    half = wrapped.astype(jnp.float32) * (math.pi / NFFT)
    sq = half * half
    sin = half * horner(sq, [(-1.0) ** k / math.factorial(2 * k + 1) for k in range(7)])
    cos = horner(sq, [(-1.0) ** k / math.factorial(2 * k) for k in range(8)])
    return 1.0 - 2.0 * sin * sin, 2.0 * sin * cos


def split(value):
    high = value.astype(jnp.bfloat16).astype(jnp.float32)
    return high, value - high


def fill_tables(bins, starts, nbins, nblock, nmode, cos_t, sin_t, cos_b, sin_b, wcat):
    lane = lax.broadcasted_iota(jnp.int32, (8, LANES), 1)
    sub = lax.broadcasted_iota(jnp.int32, (8, LANES), 0)
    row = jnp.zeros((8, LANES), jnp.int32)
    for b in range(nblock):
        row = jnp.where(lane == b, starts[b], row)
    for f in range(nbins):
        at = slice(f * nmode, (f + 1) * nmode)
        cos_b[at, :], sin_b[at, :] = turn(lax.rem(row * bins[f], NFFT))
    shape = (nbins, NFFT)
    which = lax.broadcasted_iota(jnp.int32, shape, 0)
    step = lax.broadcasted_iota(jnp.int32, shape, 1)
    number = jnp.zeros(shape, jnp.int32)
    for f in range(nbins):
        number = jnp.where(which == f, bins[f], number)
    cos, sin = turn(lax.rem(number * step, NFFT))
    for f in range(nbins):
        at = slice(f * nmode, (f + 1) * nmode)
        cos_t[at, :] = jnp.broadcast_to(cos[f:f + 1], (nmode, NFFT))
        sin_t[at, :] = jnp.broadcast_to(sin[f:f + 1], (nmode, NFFT))

    gain = 0.5 * math.sqrt(8.0 / (3.0 * NFFT))
    wave = [turn(lane + j * LANES) for j in range(NFFT // LANES)]
    length = wcat.shape[1]
    for g in range(nblock // 16):
        cols = []
        for h in range(2):
            col = jnp.zeros((8, LANES), jnp.int32)
            for i in range(8):
                col = jnp.where(sub == i, starts[g * 16 + h * 8 + i], col)
            cos_s, sin_s = turn(lax.rem(col, NFFT))
            cols.append((col, cos_s * gain, sin_s * gain))
        for j in range(length // LANES):
            ct, st = wave[j % (NFFT // LANES)]
            parts = []
            for col, cos_s, sin_s in cols:
                since = lane + j * LANES - col
                value = gain - (ct * cos_s + st * sin_s)
                parts.append(jnp.where((since >= 0) & (since < NFFT), value, 0.0))
            high, low = split(jnp.concatenate(parts, axis=0))
            high, low = high.astype(jnp.bfloat16), low.astype(jnp.bfloat16)
            at = slice(j * LANES, (j + 1) * LANES)
            for base, piece in ((0, high), (1, high), (2, low), (3, low)):
                wcat[base * nblock + g * 16:base * nblock + g * 16 + 16, at] = piece


def rotate_windows(nbins, nmode, lhs, rhs, cos_t, sin_t, store):
    for j in range(rhs.shape[1] // NFFT):
        at = slice(j * NFFT, (j + 1) * NFFT)
        b = jnp.dot(lhs, rhs[:, at], preferred_element_type=jnp.float32)
        for f in range(nbins):
            rows = slice(f * nmode, (f + 1) * nmode)
            c, s = cos_t[rows, :], sin_t[rows, :]
            re = b[2 * f * nmode:(2 * f + 1) * nmode]
            im = b[(2 * f + 1) * nmode:(2 * f + 2) * nmode]
            store(
                slice(2 * f * nmode, (2 * f + 2) * nmode),
                j,
                jnp.concatenate([c * re + s * im, c * im - s * re], axis=0),
            )


def main_kernel(dims, starts_hbm, bins_hbm, x_hbm, quad_hbm, guess_hbm,
                modes_ref, energy_ref,
                starts, bins, x_ref, quad_ref, guess_ref, xs, xr, wcat, cos_t, sin_t, cos_b, sin_b,
                lhs, a_ref, zsend, zrecv, sqsend, sqrecv, zall, scale_ref, load_sems, sems):
    (length, nvar, ctile, nblock, nbins, nmode, n_x, n_y, first, grid_points) = dims
    n = n_x * n_y
    me = lax.axis_index("sx") * n_y + lax.axis_index("sy")
    slot = me - first
    owner = jnp.logical_and(slot >= 0, slot < nbins)
    per_var = ctile // nvar
    loads = [
        pltpu.make_async_copy(src, dst, load_sems.at[i])
        for i, (src, dst) in enumerate(
            [
                (bins_hbm, bins),
                (starts_hbm, starts),
                (guess_hbm, guess_ref),
                (quad_hbm, quad_ref),
                (x_hbm, x_ref),
            ]
        )
    ]
    for load in loads:
        load.start()

    base = jnp.where(owner, slot, lax.rem(me, nbins))
    nonowner = jnp.logical_not(owner)

    def each_owner(act):
        def pick(k):
            to = lax.rem(base + k, nbins)
            where = first + to
            act(to, (where // n_y, lax.rem(where, n_y)))

        for k in range(1, nbins):
            pick(k)

        @pl.when(nonowner)
        def _():
            pick(0)

    def each_other(act):
        @pl.loop(0, n, unroll=8)
        def _(where):
            @pl.when(where != me)
            def _():
                act((where // n_y, lax.rem(where, n_y)))

    barrier = pltpu.get_barrier_semaphore()

    def greet(where):
        pl.semaphore_signal(barrier, inc=1, device_id=where, device_id_type=MESH)

    @pl.when(owner)
    def _():
        each_other(greet)

    @pl.when(nonowner)
    def _():
        each_owner(lambda to, where: greet(where))

    with jax.named_scope("tables"):
        loads[0].wait()
        loads[1].wait()
        fill_tables(bins, starts, nbins, nblock, nmode, cos_t, sin_t, cos_b, sin_b, wcat)
    with jax.named_scope("guess"):
        loads[2].wait()
        for f in range(nbins):
            rows = slice(f * nmode, (f + 1) * nmode)
            c, s = cos_b[rows, :nblock], sin_b[rows, :nblock]
            g_re, g_im = guess_ref[f, 0], guess_ref[f, 1]
            value = jnp.concatenate([g_re * c - g_im * s, g_re * s + g_im * c], axis=0)
            high, low = split(value)
            lhs[2 * f * nmode:(2 * f + 2) * nmode, :] = jnp.concatenate(
                [high, low], axis=1
            ).astype(jnp.bfloat16)
    with jax.named_scope("acoef"):
        def keep(rows, j, value):
            a_ref[rows, j * NFFT:(j + 1) * NFFT] = value.astype(jnp.bfloat16)

        rotate_windows(
            nbins, nmode, jnp.concatenate([lhs[...], lhs[...]], axis=1), wcat, cos_t, sin_t, keep
        )
    with jax.named_scope("loadwait"):
        loads[3].wait()
        loads[4].wait()
    rows = x_ref.shape[0]
    step = rows // 16

    with jax.named_scope("conv"):
        @pl.loop(0, 16)
        def _(i):
            at = pl.ds(pl.multiple_of(i * step, step), step)
            xs[at, :] = x_ref[at, :].astype(jnp.float32)

    lane = lax.broadcasted_iota(jnp.int32, (1, LANES), 1)
    with jax.named_scope("squares"):
        quads = [quad_ref[c // per_var, c % per_var:c % per_var + 1, :] for c in range(ctile)]
        total = jnp.zeros((1, LANES), jnp.float32)
        for c in range(ctile):
            col = xs[pl.ds(c, length, stride=ctile), :]
            xr[:, c * LANES:(c + 1) * LANES] = col.astype(jnp.bfloat16)
            sums = jnp.sum(col * col, axis=0, keepdims=True) * quads[c]
            one = jnp.sum(sums, axis=1, keepdims=True)
            total = total + jnp.where(lane == c // per_var, one, 0.0)

        sqsend[...] = total

    def send(src, dst, number):
        each_owner(
            lambda to, where: pltpu.make_async_remote_copy(
                src_ref=src(to),
                dst_ref=dst,
                send_sem=sems.at[2 * number],
                recv_sem=sems.at[2 * number + 1],
                device_id=where,
                device_id_type=MESH,
            ).start()
        )

    low_half = lax.broadcasted_iota(jnp.int32, (nmode, LANES), 1) < nblock
    span = per_var * LANES
    for v in range(nvar):
        with jax.named_scope(f"var{v}"):
            at = slice(v * span, (v + 1) * span)
            weight = jnp.concatenate(quads[v * per_var:(v + 1) * per_var], axis=1)
            u = jnp.dot(a_ref[...], xr[:, at], preferred_element_type=jnp.float32)
            u = (u * weight).astype(jnp.bfloat16)
            acc = None
            for j in range(length // NFFT):
                steps = slice(j * NFFT, (j + 1) * NFFT)
                back = lax.dot_general(
                    u, xr[steps, at], (((1,), (1,)), ((), ())),
                    preferred_element_type=jnp.float32,
                )
                turned = []
                for f in range(nbins):
                    rows = slice(f * nmode, (f + 1) * nmode)
                    c, s = cos_t[rows, :], sin_t[rows, :]
                    re = back[2 * f * nmode:(2 * f + 1) * nmode]
                    im = back[(2 * f + 1) * nmode:(2 * f + 2) * nmode]
                    turned.append(
                        jnp.concatenate([c * re - s * im, s * re + c * im], axis=0).astype(
                            jnp.bfloat16
                        )
                    )
                one = lax.dot_general(
                    jnp.concatenate(turned, axis=0), wcat[nblock:3 * nblock, steps],
                    (((1,), (1,)), ((), ())), preferred_element_type=jnp.float32,
                )
                acc = one if acc is None else acc + one
            acc = (acc + pltpu.roll(acc, nblock, 1)) * (1.0 / (3.0 * grid_points))
            for f in range(nbins):
                re = slice(2 * f * nmode, (2 * f + 1) * nmode)
                im = slice((2 * f + 1) * nmode, (2 * f + 2) * nmode)
                zsend[v, f] = jnp.where(low_half, acc[re], acc[im]).astype(jnp.bfloat16)
        if v == 0:
            with jax.named_scope("barrier"):
                pl.semaphore_wait(barrier, jnp.where(owner, n - 1, nbins))
            send(lambda to: sqsend, sqrecv.at[me], nvar)
        with jax.named_scope("send"):
            send(lambda to, v=v: zsend.at[v, to], zrecv.at[v, me], v)

    gathered = 2 * nvar + 2
    def wait_for(ref, sem):
        pltpu.make_async_copy(ref, ref, sems.at[sem]).wait()

    half = nbins // 2

    @pl.when(owner)
    def _():
        with jax.named_scope("a2a"):
            wait_for(sqrecv.at[pl.ds(0, n - 1)], 2 * nvar + 1)
            sqrecv[me] = sqsend[...]
            total = jnp.sum(sqrecv[...], axis=0)
            scale = lax.rsqrt(total / (length * grid_points) + EPS)
            scale_ref[...] = scale
            square = scale * scale
            z = jnp.zeros((nmode, LANES), jnp.float32)
            for v in range(nvar):
                wait_for(zrecv.at[v, pl.ds(0, n - 1)], 2 * v + 1)
                zrecv[v, me] = zsend[v, slot]
                factor = jnp.sum(jnp.where(lane == v, square, 0.0), axis=1, keepdims=True)
                z = z + jnp.sum(zrecv[v].astype(jnp.float32), axis=0) * factor
        with jax.named_scope("zsum"):
            zall[slot] = z.astype(jnp.bfloat16)
        with jax.named_scope("agsend"):
            each_other(
                lambda where: pltpu.make_async_remote_copy(
                    src_ref=zall.at[slot],
                    dst_ref=zall.at[slot],
                    send_sem=sems.at[gathered],
                    recv_sem=sems.at[gathered + 1 + slot // half],
                    device_id=where,
                    device_id_type=MESH,
                ).start()
            )
            for k in range((n - nbins) // nbins):
                rank = slot + k * nbins
                where = jnp.where(rank < first, rank, rank + nbins)
                pltpu.make_async_remote_copy(
                    src_ref=scale_ref,
                    dst_ref=scale_ref,
                    send_sem=sems.at[gathered + 3],
                    recv_sem=sems.at[gathered + 4],
                    device_id=(where // n_y, lax.rem(where, n_y)),
                    device_id_type=MESH,
                ).start()

    roots = [jnp.sqrt(quads[c]) for c in range(ctile)]
    count = half * nmode
    column = lax.broadcasted_iota(jnp.int32, (nmode, nbins), 1)

    def finish(group):
        mine = jnp.logical_and(owner, slot // half == group)

        with jax.named_scope("agwait"):
            @pl.when(mine)
            def _():
                wait_for(zall.at[pl.ds(0, half - 1)], gathered + 1 + group)

            @pl.when(jnp.logical_not(mine))
            def _():
                wait_for(zall.at[pl.ds(0, half)], gathered + 1 + group)

        with jax.named_scope("macoef"):
            rows_l = []
            energy = energy_ref[...]
            for i in range(half):
                f = group * half + i
                z = zall[f].astype(jnp.float32)
                norms = jnp.sum(z * z, axis=1, keepdims=True)
                energy = jnp.where(column == f, jnp.sqrt(norms / nblock), energy)
                coef = z * lax.rsqrt(norms + EPS)
                swapped = pltpu.roll(coef, nblock, 1)
                rows_l.append(
                    jnp.concatenate(
                        [jnp.where(low_half, coef, swapped), jnp.where(low_half, swapped, coef)],
                        axis=0,
                    ).astype(jnp.bfloat16)
                )
            energy_ref[...] = energy

            def keep(rows, j, value):
                high, low = split(value)
                at = slice(j * NFFT, (j + 1) * NFFT)
                a_ref[rows, at] = high.astype(jnp.bfloat16)
                a_ref[slice(2 * count + rows.start, 2 * count + rows.stop), at] = low.astype(
                    jnp.bfloat16
                )

            table = pl.ds(pl.multiple_of(group * count, count), count)
            rotate_windows(
                half, nmode, jnp.concatenate(rows_l, axis=0), wcat.at[nblock:3 * nblock],
                cos_t.at[table], sin_t.at[table], keep
            )
        return mine

    def multiply(group, scales):
        with jax.named_scope("mdot"):
            for v in range(nvar):
                at = slice(v * span, (v + 1) * span)
                m = jnp.dot(a_ref[...], xr[:, at], preferred_element_type=jnp.float32)
                m = m[:2 * count] + m[2 * count:]
                for k in range(per_var):
                    c = v * per_var + k
                    modes_ref[pl.ds(group * (2 * count * ctile) + c, 2 * count, stride=ctile), :] = (
                        m[:, k * LANES:(k + 1) * LANES] * (scales[v] * roots[c])
                    )

    energy_ref[...] = jnp.zeros((nmode, nbins), jnp.float32)
    near = jnp.where(me < n // 2, 0, 1)
    with jax.named_scope("scalewait"):
        @pl.when(nonowner)
        def _():
            wait_for(scale_ref, gathered + 4)
    scale = scale_ref[...]
    scales = [jnp.sum(jnp.where(lane == v, scale, 0.0), axis=1, keepdims=True) for v in range(nvar)]

    @pl.loop(0, 2)
    def _(i):
        group = jnp.where(i == 0, near, 1 - near)
        finish(group)
        multiply(group, scales)

    with jax.named_scope("drain"):
        @pl.when(owner)
        def _():
            for v in range(nvar):
                wait_for(zsend.at[v, pl.ds(0, nbins - 1)], 2 * v)
            wait_for(sqrecv.at[pl.ds(0, nbins - 1)], 2 * nvar)
            for _ in range((n - 1) // nbins):
                wait_for(zall, gathered)
            rest = (n - 1) % nbins
            if rest:
                wait_for(zall.at[pl.ds(0, rest)], gathered)
            for _ in range((n - nbins) // nbins):
                wait_for(scale_ref, gathered + 3)

        @pl.when(nonowner)
        def _():
            for v in range(nvar):
                wait_for(zsend.at[v], 2 * v)
            wait_for(sqrecv.at[pl.ds(0, nbins)], 2 * nvar)


def copy_kernel(pieces, value, energy, out_hbm, energy_hbm, sems):
    size = value.shape[0] // pieces
    copies = [
        pltpu.make_async_copy(
            value.at[pl.ds(i * size, size)], out_hbm.at[pl.ds(i * size, size)], sems.at[i]
        )
        for i in range(pieces)
    ]
    copies.append(pltpu.make_async_copy(energy, energy_hbm, sems.at[pieces]))
    for copy in copies:
        copy.start()
    for copy in copies:
        copy.wait()


def shards(n_x, n_y, snapshots, quad_weight, mode_guess, bins, starts):
    length, nvar, cols_x, cols_y = snapshots.shape
    nbins = bins.shape[0]
    nblock = starts.shape[0]
    nmode = mode_guess.shape[-1]
    ctile = nvar * cols_x
    points = ctile * cols_y
    n = n_x * n_y
    grid_points = cols_x * cols_y * n
    vmem = pl.BlockSpec(memory_space=pltpu.VMEM)
    hbm = pl.BlockSpec(memory_space=pltpu.HBM)
    limit = 30 * 1024 * 1024
    rows = 2 * nbins * nmode

    x = snapshots.reshape(length * ctile, cols_y)
    guess = jnp.transpose(mode_guess, (0, 2, 3, 1))

    operands = [
        pltpu.with_memory_space_constraint(value, pltpu.HBM)
        for value in (starts, bins, x, quad_weight, guess)
    ]
    first = (n - nbins) // 2
    dims = (length, nvar, ctile, nblock, nbins, nmode, n_x, n_y, first, grid_points)
    modes, energy = pl.pallas_call(
        functools.partial(main_kernel, dims),
        name="spod",
        out_shape=(
            jax.ShapeDtypeStruct((rows * ctile, cols_y), jnp.float32),
            jax.ShapeDtypeStruct((nmode, nbins), jnp.float32),
        ),
        in_specs=[hbm] * 5,
        out_specs=(vmem, vmem),
        scratch_shapes=[
            pltpu.SMEM(starts.shape, jnp.int32),
            pltpu.SMEM(bins.shape, jnp.int32),
            pltpu.VMEM(x.shape, jnp.bfloat16),
            pltpu.VMEM(quad_weight.shape, jnp.float32),
            pltpu.VMEM(guess.shape, jnp.float32),
            pltpu.VMEM((length * ctile, cols_y), jnp.float32),
            pltpu.VMEM((length, points), jnp.bfloat16),
            pltpu.VMEM((4 * nblock, length), jnp.bfloat16),
            pltpu.VMEM((nbins * nmode, NFFT), jnp.float32),
            pltpu.VMEM((nbins * nmode, NFFT), jnp.float32),
            pltpu.VMEM((nbins * nmode, LANES), jnp.float32),
            pltpu.VMEM((nbins * nmode, LANES), jnp.float32),
            pltpu.VMEM((rows, 2 * nblock), jnp.bfloat16),
            pltpu.VMEM((rows, length), jnp.bfloat16),
            pltpu.VMEM((nvar, nbins, nmode, LANES), jnp.bfloat16),
            pltpu.VMEM((nvar, n, nmode, LANES), jnp.bfloat16),
            pltpu.VMEM((1, LANES), jnp.float32),
            pltpu.VMEM((n, 1, LANES), jnp.float32),
            pltpu.VMEM((nbins, nmode, LANES), jnp.bfloat16),
            pltpu.VMEM((1, LANES), jnp.float32),
            pltpu.SemaphoreType.DMA((5,)),
            pltpu.SemaphoreType.DMA((2 * nvar + 7,)),
        ],
        compiler_params=pltpu.CompilerParams(
            collective_id=0, has_side_effects=True, vmem_limit_bytes=limit
        ),
    )(*operands)

    pieces = 1
    modes, energy = pl.pallas_call(
        functools.partial(copy_kernel, pieces),
        name="store",
        out_shape=(
            jax.ShapeDtypeStruct(modes.shape, jnp.float32),
            jax.ShapeDtypeStruct(energy.shape, jnp.float32),
        ),
        in_specs=[vmem, vmem],
        out_specs=(hbm, hbm),
        scratch_shapes=[pltpu.SemaphoreType.DMA((pieces + 1,))],
        compiler_params=pltpu.CompilerParams(vmem_limit_bytes=limit),
    )(modes, energy)
    return (
        modes.reshape(nbins, 2, nmode, nvar, cols_x, cols_y),
        energy.T,
    )


def solution(mesh):
    n_x, n_y = mesh.shape["sx"], mesh.shape["sy"]
    return jax.shard_map(
        functools.partial(shards, n_x, n_y),
        mesh=mesh,
        in_specs=(P(None, None, "sx", "sy"), P(None, "sx", "sy"), P(), P(), P()),
        out_specs=(P(None, None, None, None, "sx", "sy"), P()),
        check_vma=False,
    )
```
